32 devices in a mesh: beam: 2 (over x), wide: 16 (over z, y, core).
Axes of the slice: x: 2, y: 2, z: 4, core: 2. Of those that a mesh axis runs over, the one named last changes fastest.
Arguments:
- filterbank: bfloat16 [2, 4096, 4096], P('beam', 'wide'), parts along dimension 0, may hold values from -100 to 100
- channel_mask: int32 [8192], P(('beam', 'wide')), parts along dimension 0, may hold values 0 or 1
- band_edges: int32 [7], replicated, may hold values from 385 to 3711, as said below
- dm_delays: int32 [16], replicated, may hold values from 0 to 2047
Outputs:
- series: float32 [2, 16, 4096], P('beam', 'wide'), parts along dimension 0
The draws below stay inside these ranges and needn't reach their ends.
There are 2 independent parts, one for each index of `beam`. The reference program is written for one: setup_inputs(seed, part) draws one part's arguments, and reference() takes and returns one part's arrays. A program takes and returns all parts, laid end to end along the dimension named above; an argument that names none is the same for every part. Nothing has to cross between parts.
Inputs may be any that keep to these rules, and one draw needn't show every extreme that they name: `band_edges`: strictly increasing; entry i lies at (i + 1) * 512 up to a shift of less than 128.
All inputs are finite; a program needn't handle non-finite values. No bound on the sum of `channel_mask` on one device may be relied on, other than what follows from the above.
Results may differ from the reference program's by a relative error of at most 0.0063.
Values may be sent and summed in bfloat16 or wider, within the bound.
A program may use at most 64 MiB of HBM per device.

```python
import math
import jax
import jax.numpy as jnp
from jax import lax

C = 4096
NT = 4096
NBLK = 8
NB = 1
NDM = 16
NBAND = 8


def draw_filterbank(key, part):
    key_noise, key_gain, key_time, key_ripple = jax.random.split(key, 4)
    channel_pos = jnp.arange(C, dtype=jnp.float32)
    ramp = 1.0 + 2.0 * channel_pos / (C - 1)
    offset = jax.random.uniform(key_ripple, (), minval=0.0, maxval=2.0 * math.pi)
    ripple = jnp.exp(jnp.sin(2.0 * math.pi * channel_pos * NBAND / (3.0 * C) + offset))
    noise = jax.random.normal(key_noise, (NB, C, NT))
    gain = jnp.exp(jax.random.uniform(key_gain, (C,)) * math.log(10.0))
    time_scale = jnp.exp(jax.random.uniform(key_time, (NB, 1, NT)) * math.log(10.0))
    values = noise * (ramp * ripple * gain)[None, :, None] * time_scale / 20.0
    return jnp.clip(values, -100.0, 100.0).astype(jnp.bfloat16)


def draw_band_edges(key, part):
    spacing = C // NBAND
    jitter = C // (4 * NBAND)
    offsets = jax.random.randint(key, (NBAND - 1,), -(jitter - 1), jitter)
    offsets = offsets.at[0].set(-(jitter - 1)).at[NBAND - 2].set(jitter - 1)
    return (jnp.arange(1, NBAND, dtype=jnp.int32) * spacing + offsets).astype(jnp.int32)


def plant(values, key, least, top_value):
    longest = values.shape.index(max(values.shape))
    spots = []
    for shift in (0, 1):
        where = [jax.random.randint(jax.random.fold_in(key, axis), (), 0, length) for axis, length in enumerate(values.shape)]
        where[longest] = (where[longest] + shift) % values.shape[longest]
        spots.append(tuple(where))
    return values.at[spots[0]].set(least).at[spots[1]].set(top_value)


def setup_inputs(seed: int = 0, part: int = 0) -> dict:
    seeds = jax.random.split(jax.random.key(seed), 5)
    own_keys = jax.random.split(jax.random.fold_in(seeds[4], part), 5)
    return {
        "filterbank": draw_filterbank(jax.random.fold_in(jax.random.fold_in(seeds[4], part), 71), part),
        "channel_mask": plant((jax.random.randint(own_keys[1], (C,), 0, 8) < 7).astype(jnp.int32), jax.random.fold_in(own_keys[1], 1), 0, 1),
        "band_edges": draw_band_edges(jax.random.fold_in(seeds[4], 71), part),
        "dm_delays": plant(jax.random.randint(seeds[3], (NDM,), 0, NT // 2), jax.random.fold_in(seeds[3], 1), 0, (NT // 2) - 1).astype(jnp.int32),
    }


def delay_fractions(first_channel, channel_count, total_channels):
    channel_ids = first_channel + jnp.arange(channel_count, dtype=jnp.int32)
    ratio = 0.5 + 0.5 * (channel_ids.astype(jnp.float32) + 0.5) / total_channels
    return (1.0 / (ratio * ratio) - 1.0) / 3.0

def noise_floors(band_power, band_edges, channels):
    bounds = jnp.concatenate([jnp.zeros((1,), jnp.int32), band_edges.astype(jnp.int32), jnp.full((1,), channels, jnp.int32)])
    widths = (bounds[1:] - bounds[:-1]).astype(jnp.float32)
    return jnp.sqrt(band_power / widths[None, :, None] + 1e-05)

def forward_tables(first_bin, bin_count, samples):
    bin_ids = first_bin + jnp.arange(bin_count, dtype=jnp.int32)
    times = jnp.arange(samples, dtype=jnp.int32)
    product = bin_ids[:, None] * times[None, :] % samples
    angle = product.astype(jnp.float32) * (2.0 * math.pi / samples)
    tables = jnp.stack([jnp.cos(angle), -jnp.sin(angle)], axis=0)
    return tables.reshape(2 * bin_count, samples).astype(jnp.bfloat16)

def inverse_tables(first_bin, bin_count, samples, channels):
    bin_ids = first_bin + jnp.arange(bin_count, dtype=jnp.int32)
    times = jnp.arange(samples, dtype=jnp.int32)
    product = bin_ids[:, None] * times[None, :] % samples
    angle = product.astype(jnp.float32) * (2.0 * math.pi / samples)
    weight = jnp.where(bin_ids == 0, 1.0, 2.0).astype(jnp.float32) / (samples * math.sqrt(channels))
    tables = jnp.stack([weight[:, None] * jnp.cos(angle), -weight[:, None] * jnp.sin(angle)], axis=1)
    return tables.reshape(2 * bin_count, samples).astype(jnp.bfloat16)

def phase_tables(first_bin, bin_count, fractions, dm_delays, samples):
    bin_ids = first_bin + jnp.arange(bin_count, dtype=jnp.int32)
    cycles = (bin_ids[:, None] * dm_delays[None, :]).astype(jnp.float32)
    angle = cycles[:, None, :] * fractions[None, :, None] * (2.0 * math.pi / samples)
    return (jnp.cos(angle).astype(jnp.bfloat16), jnp.sin(angle).astype(jnp.bfloat16))

def dedisperse_block(spec_real, spec_imag, cos_tab, sin_tab):
    spec_real = spec_real.astype(jnp.float32)
    spec_imag = spec_imag.astype(jnp.float32)
    cos_tab = cos_tab.astype(jnp.float32)
    sin_tab = sin_tab.astype(jnp.float32)
    real_part = jnp.einsum('fbc,fcd->fbd', spec_real, cos_tab) - jnp.einsum('fbc,fcd->fbd', spec_imag, sin_tab)
    imag_part = jnp.einsum('fbc,fcd->fbd', spec_real, sin_tab) + jnp.einsum('fbc,fcd->fbd', spec_imag, cos_tab)
    return jnp.stack([real_part, imag_part], axis=1)

def reference(filterbank, channel_mask, band_edges, dm_delays):
    beams, channels, samples = filterbank.shape
    bands = band_edges.shape[0] + 1
    signal = filterbank.astype(jnp.float32).reshape(beams, channels, NBLK, samples // NBLK)
    power = lax.optimization_barrier(jnp.mean(signal * signal, axis=3))
    channel_ids = jnp.arange(channels, dtype=jnp.int32)
    band_ids = lax.optimization_barrier(jnp.sum((band_edges[None, :] <= channel_ids[:, None]).astype(jnp.int32), axis=1))
    member = (band_ids[:, None] == jnp.arange(bands, dtype=jnp.int32)[None, :]).astype(jnp.float32)
    keep = channel_mask.astype(jnp.float32)
    band_power = jnp.einsum('cj,bck->bjk', member * keep[:, None], power, precision=lax.Precision.HIGHEST)
    floors = noise_floors(band_power, band_edges, channels)
    channel_floor = jnp.einsum('cj,bjk->bck', member, floors, precision=lax.Precision.HIGHEST)
    cleaned = (signal / channel_floor[..., None] * keep[None, :, None, None]).reshape(beams, channels, samples).astype(jnp.bfloat16)
    rows_flat = cleaned.reshape(beams * channels, samples)
    rows_turned = rows_flat.T
    bins = samples // 4
    dft_step = math.gcd(bins, 256)

    def spectrum_part(first_bin):
        tables = forward_tables(first_bin, dft_step, samples)
        block = jnp.dot(tables, rows_turned, preferred_element_type=jnp.float32).astype(jnp.bfloat16)
        return block.reshape(2, dft_step, beams, channels)
    firsts = jnp.arange(bins // dft_step, dtype=jnp.int32) * dft_step
    blocks = lax.map(spectrum_part, firsts)
    spectrum = jnp.transpose(blocks, (1, 0, 2, 3, 4)).reshape(2, bins, beams, channels)
    fractions = delay_fractions(0, channels, channels)
    phase_step = math.gcd(bins, 8)

    def dm_part(first_bin):
        spec_part = lax.dynamic_slice_in_dim(spectrum, first_bin, phase_step, 1)
        cos_tab, sin_tab = phase_tables(first_bin, phase_step, fractions, dm_delays, samples)
        return dedisperse_block(spec_part[0], spec_part[1], cos_tab, sin_tab)
    phase_firsts = jnp.arange(bins // phase_step, dtype=jnp.int32) * phase_step
    dm_blocks = lax.map(dm_part, phase_firsts)
    trials = dm_delays.shape[0]
    dm_spectrum = dm_blocks.reshape(bins, 2, beams, trials).astype(jnp.bfloat16)
    flat = dm_spectrum.reshape(bins * 2, beams * trials)
    table = inverse_tables(0, bins, samples, channels)
    series = jnp.dot(flat.T, table, preferred_element_type=jnp.float32)
    return series.reshape(beams, trials, samples)
```

```python
import functools
import math

import jax
import jax.numpy as jnp
import ml_dtypes
import numpy as np
from jax import lax
from jax.experimental import pallas as pl
from jax.experimental.pallas import tpu as pltpu
from jax.sharding import PartitionSpec as P

NBLK = 8
LANES = 128
VMEM = pl.BlockSpec(memory_space=pltpu.VMEM)
HBM = pl.BlockSpec(memory_space=pltpu.HBM)
MESH = pl.DeviceIdType.MESH
F32 = jnp.float32
BF16 = jnp.bfloat16


def turn_coefficients():
    degree = 5
    nodes = np.cos((np.arange(64) + 0.5) * np.pi / 64) * 0.125 + 0.125
    root = np.sqrt(nodes)
    cos_fit = np.polynomial.Chebyshev.fit(nodes, np.cos(2 * np.pi * root), degree, domain=[0, 0.25])
    sin_fit = np.polynomial.Chebyshev.fit(
        nodes, np.sin(2 * np.pi * root) / root, degree, domain=[0, 0.25]
    )
    as_power = lambda fit: [float(np.float32(v)) for v in fit.convert(kind=np.polynomial.Polynomial).coef]
    return as_power(cos_fit), as_power(sin_fit)


COS_COEF, SIN_COEF = turn_coefficients()


def cos_sin_turns(turns):
    r = turns - jnp.floor(turns + 0.5)
    s = r * r
    c = jnp.full_like(s, COS_COEF[-1])
    q = jnp.full_like(s, SIN_COEF[-1])
    for a, b in zip(COS_COEF[-2::-1], SIN_COEF[-2::-1]):
        c = c * s + a
        q = q * s + b
    return c, q * r


def forward_table(samples):
    window = samples // NBLK
    blocks = samples // 4 // 64
    r = np.arange(8)[:, None, None]
    g = 8 * np.arange(blocks)[None, :, None] + (np.arange(8)[None, None, :] ^ r)
    f = 8 * g + r
    angle = (f[..., None] * np.arange(window) % samples) * (2 * np.pi / samples)
    table = np.stack([np.cos(angle), -np.sin(angle)], axis=2)
    return table.reshape(8 * blocks * 16, window).astype(ml_dtypes.bfloat16)


def inverse_tables(samples):
    window = samples // 8
    groups = samples // 32
    g = np.arange(groups)
    t = np.arange(window)
    angle = (g[:, None] * t[None, :] % window) * (2 * np.pi / window)
    c, s = np.cos(angle), np.sin(angle)
    real = np.concatenate([c, s], axis=1).reshape(groups // 8, 8, 2 * window)
    imag = np.concatenate([-s, c], axis=1).reshape(groups // 8, 8, 2 * window)
    first = np.stack([real, imag], axis=1).reshape(2 * groups, 2 * window)
    turn = np.arange(8)[:, None] * t[None, :] * (2 * np.pi / samples)
    twist = np.concatenate([np.cos(turn), np.sin(turn)], axis=0)
    return first.astype(ml_dtypes.bfloat16), twist.astype(np.float32)


def partner(me, step, n):
    if n & (n - 1):
        return lax.rem(me + step, n)
    out, bit = 0, 1
    while bit < n:
        out = out + lax.rem(me // bit + step // bit, 2) * bit
        bit *= 2
    return out


def untangle(x):
    row = lax.broadcasted_iota(jnp.int32, x.shape, 0)
    lane = lax.broadcasted_iota(jnp.int32, x.shape, 1)
    for s in (1, 2, 4):
        low_row, low_lane = (row & s) == 0, (lane & s) == 0
        up = pltpu.roll(x, 8 - s, 0)
        right = pltpu.roll(x, s, 1)
        cross = pltpu.roll(pltpu.roll(x, LANES - s, 1), s, 0)
        x = jnp.where(low_row, jnp.where(low_lane, x, up), jnp.where(low_lane, cross, right))
    return x


def fused_kernel(
    n, bands, channels, trials,
    edges_hbm, delays_hbm, mask_hbm, x_hbm, tab_hbm, inv_hbm, twist_hbm,
    out_ref,
    edges_ref, delays_ref, mask_ref, x_ref, tab_ref, inv_ref, twist_ref, sq_ref, rot_c, rot_s, base_c, base_s,
    y_ref, spec_ref, pick_ref, scale_ref, own_power, got_power, part_ref, got_part,
    small_sem, x_sem, table_sem, power_send, power_recv, part_send, part_recv,
):
    local, samples = x_ref.shape
    window = samples // NBLK
    blocks = samples // 4 // 64
    share = out_ref.shape[0]
    gs = LANES // trials
    halves = 8 // gs
    assert gs * trials == LANES and halves * gs == 8 and 16 * blocks == 2 * LANES
    assert bands * NBLK <= LANES
    me = lax.axis_index("wide")
    first = me * local

    small = [
        pltpu.make_async_copy(src, dst, small_sem.at[i])
        for i, (src, dst) in enumerate(
            [(delays_hbm, delays_ref), (edges_hbm, edges_ref), (mask_hbm, mask_ref)]
        )
    ]
    for copy in small:
        copy.start()
    rows = 64

    def load(i):
        at = pl.ds(pl.multiple_of(i * rows, rows), rows)
        return pltpu.make_async_copy(x_hbm.at[at], x_ref.at[at], x_sem.at[i])

    for i in range(local // rows):
        load(i).start()

    barrier = pltpu.get_barrier_semaphore()
    for step in range(1, n):
        pl.semaphore_signal(
            barrier, inc=1, device_id={"wide": lax.rem(me + step, n)}, device_id_type=MESH
        )

    tables = [
        pltpu.make_async_copy(src, dst, table_sem.at[i])
        for i, (src, dst) in enumerate(
            [(tab_hbm, tab_ref), (inv_hbm, inv_ref), (twist_hbm, twist_ref)]
        )
    ]
    for copy in tables:
        copy.start()
    for copy in small:
        copy.wait()

    lane = lax.broadcasted_iota(jnp.int32, (1, LANES), 1)
    delay_row = jnp.zeros((1, LANES), F32)
    for d in range(trials):
        delay_row = jnp.where(lane // gs == d, delays_ref[d].astype(F32), delay_row)
    delay_row = delay_row * (1.0 / samples)
    offset_row = (lane % gs).astype(F32) * 8.0 + 3.5
    prow = 32

    def phases(i, carry):
        at = pl.ds(pl.multiple_of(i * prow, prow), prow)
        channel = first + i * prow + lax.broadcasted_iota(jnp.int32, (prow, LANES), 0)
        ratio = 0.5 + 0.5 * (channel.astype(F32) + 0.5) / channels
        sweep = (1.0 / (ratio * ratio) - 1.0) / 3.0 * delay_row
        half_c, half_s = cos_sin_turns(sweep * 0.5)
        twice = 4.0 * half_c * half_c - 2.0
        before, now = (half_c, -half_s), (half_c, half_s)
        for k in range(4):
            if k:
                before, now = now, tuple(twice * v - u for u, v in zip(before, now))
            rot_c[k, at, :] = now[0]
            rot_s[k, at, :] = now[1]
        step_c, step_s = cos_sin_turns(sweep * (8.0 * gs))
        a, b = cos_sin_turns(sweep * offset_row)
        old = (a * step_c + b * step_s, b * step_c - a * step_s)
        now = (a, b)
        double = step_c + step_c
        for k in range(blocks * halves):
            base_c[k, at, :] = now[0]
            base_s[k, at, :] = now[1]
            old, now = now, tuple(double * v - u for u, v in zip(old, now))
        return carry

    lax.fori_loop(0, local // prow // 2, phases, 0)

    def square(i, carry):
        load(i).wait()
        at = pl.ds(pl.multiple_of(i * rows, rows), rows)
        for k in range(NBLK):
            total = None
            for p in range(window // LANES):
                v = x_ref[at, pl.ds(k * window + p * LANES, LANES)].astype(F32)
                total = v * v if total is None else total + v * v
            sq_ref[at, pl.ds(k * LANES, LANES)] = total.astype(BF16)
        return carry

    lax.fori_loop(0, local // rows, square, 0)
    channel_row = first + lax.broadcasted_iota(jnp.int32, (1, local), 1)
    keep = mask_ref[...].astype(F32)
    picks = []
    for j in range(bands):
        inside = channel_row < (channels if j == bands - 1 else edges_ref[j])
        if j:
            inside = jnp.logical_and(inside, channel_row >= edges_ref[j - 1])
        picks.append(jnp.where(inside, keep, 0.0))
    pick = jnp.concatenate(picks, axis=0).astype(BF16)
    summed = jnp.dot(pick, sq_ref[...], preferred_element_type=F32)
    spot = lax.broadcasted_iota(jnp.int32, (bands, LANES), 1)
    band_row = lax.broadcasted_iota(jnp.int32, (bands, LANES), 0)
    powers = jnp.zeros((bands, LANES), F32)
    for k in range(NBLK):
        part = jnp.sum(summed[:, k * LANES : (k + 1) * LANES], axis=1, keepdims=True)
        powers = jnp.where(spot == band_row * NBLK + k, part, powers)
    own_power[...] = jnp.sum(powers, axis=0, keepdims=True) * (1.0 / window)

    pl.semaphore_wait(barrier, n - 1)
    power_copies = []
    for step in range(n - 1, 0, -1):
        copy = pltpu.make_async_remote_copy(
            src_ref=own_power,
            dst_ref=got_power.at[step],
            send_sem=power_send.at[step],
            recv_sem=power_recv.at[step],
            device_id={"wide": partner(me, step, n)},
            device_id_type=MESH,
        )
        copy.start()
        power_copies.append(copy)

    lax.fori_loop(local // prow // 2, local // prow, phases, 0)
    pick_ref[...] = jnp.transpose(jnp.broadcast_to(keep, (LANES, local)))
    tables[0].wait()

    total = own_power[...]
    for step in range(n - 1, 0, -1):
        power_copies[n - 1 - step].wait()
        total = total + got_power[step]
    width = jnp.zeros((1, LANES), jnp.int32)
    for j in range(bands):
        high = channels if j == bands - 1 else edges_ref[j]
        low = edges_ref[j - 1] if j else 0
        width = jnp.where(lane // NBLK == j, high - low, width)
    width = jnp.maximum(width, 1).astype(F32)
    level = 1.0 / jnp.sqrt(total / width + 1e-05)

    levels = [
        jnp.broadcast_to(pltpu.roll(level, LANES - NBLK * j, 1) if j else level, (8, LANES))
        for j in range(bands)
    ]
    for t in range(local // 8):
        at = slice(8 * t, 8 * t + 8)
        channel = first + 8 * t + lax.broadcasted_iota(jnp.int32, (8, LANES), 0)
        scale = levels[-1]
        for j in range(bands - 2, -1, -1):
            scale = jnp.where(channel < edges_ref[j], levels[j], scale)
        scale = scale * pick_ref[at, :]
        for m in range(NBLK):
            scale_ref[m, at, :] = jnp.broadcast_to(scale[:, m : m + 1], (8, LANES))

    crow = 16

    def fold(i, carry):
        at = pl.ds(pl.multiple_of(i * crow, crow), crow)
        columns = [scale_ref[m, at, :] for m in range(8)]
        root = math.sqrt(0.5)
        for p in range(window // LANES):
            here = slice(p * LANES, (p + 1) * LANES)
            x = [
                x_ref[at, m * window + p * LANES : m * window + (p + 1) * LANES].astype(F32)
                * columns[m]
                for m in range(8)
            ]
            plus = [x[m] + x[m + 4] for m in range(4)]
            minus = [x[m] - x[m + 4] for m in range(4)]
            even, odd = plus[0] + plus[2], plus[1] + plus[3]
            near, far = root * (minus[1] - minus[3]), root * (minus[1] + minus[3])
            folded = (
                even + odd, even - odd,
                minus[0] + near, -(far + minus[2]),
                plus[0] - plus[2], plus[3] - plus[1],
                minus[0] - near, minus[2] - far,
            )
            for k, value in enumerate(folded):
                y_ref[k, at, here] = value.astype(BF16)
        return carry

    lax.fori_loop(0, local // crow, fold, 0, unroll=2)

    def product(which, r):
        both = lax.dot_general(
            tab_ref[r * 16 * blocks : (r + 1) * 16 * blocks, :], y_ref[which],
            (((1,), (1,)), ((), ())), preferred_element_type=F32,
        ).reshape(blocks, 2, 8, local)
        return both[:, 0], both[:, 1]

    for r in range(8):
        if r % 4 == 0:
            re, im = product(r // 4, r)
        else:
            kind = min(r, 8 - r)
            (a_re, a_im), (b_re, b_im) = product(2 * kind, r), product(2 * kind + 1, r)
            if r < 4:
                re, im = a_re - b_im, a_im + b_re
            else:
                re, im = a_re + b_im, a_im - b_re
        spec_ref[r] = jnp.concatenate([re, im], axis=1).astype(BF16)

    row8 = lax.broadcasted_iota(jnp.int32, (8, LANES), 0)
    lane8 = lax.broadcasted_iota(jnp.int32, (8, LANES), 1) % gs
    kept = [[[] for _ in range(2)] for _ in range(halves)]
    for block in range(blocks):
        for h in range(halves):
            code = row8 ^ (lane8 + h * gs)
            xa, xb = base_c[block * halves + h], base_s[block * halves + h]
            got_re = got_im = jnp.zeros((8, LANES), F32)
            for k in range(4):
                c, s = rot_c[k], rot_s[k]
                moving = jnp.concatenate([spec_ref[3 - k, block], spec_ref[4 + k, block]], axis=0)
                one = jnp.dot(moving, jnp.concatenate([(xa * c).astype(BF16), (xb * s).astype(BF16)], axis=1), preferred_element_type=F32)
                two = jnp.dot(moving, jnp.concatenate([(xa * s).astype(BF16), (xb * c).astype(BF16)], axis=1), preferred_element_type=F32)
                ac, bs, as_, bc = one[:, :LANES], one[:, LANES:], two[:, :LANES], two[:, LANES:]
                re, im = slice(0, 8), slice(8, 16)
                out_re = (ac[re] + bs[re]) - (bc[im] - as_[im])
                out_im = (bc[re] - as_[re]) + (ac[im] + bs[im])
                got_re = jnp.where(code == 3 - k, out_re, got_re)
                got_im = jnp.where(code == 3 - k, out_im, got_im)
                re, im = slice(16, 24), slice(24, 32)
                out_re = (ac[re] - bs[re]) - (as_[im] + bc[im])
                out_im = (as_[re] + bc[re]) + (ac[im] - bs[im])
                got_re = jnp.where(code == 4 + k, out_re, got_re)
                got_im = jnp.where(code == 4 + k, out_im, got_im)
            kept[h][2 * block // blocks].append(jnp.concatenate([got_re, got_im], axis=0))
    turned = [[jnp.transpose(jnp.concatenate(v, axis=0)) for v in pair] for pair in kept]
    for d in range(trials):
        at = slice(d * gs, (d + 1) * gs)
        pieces = [turned[h][side][at] for side in range(2) for h in range(halves)]
        part_ref[d] = jnp.concatenate(pieces, axis=0).astype(BF16)

    def part_copy(step):
        to = partner(me, step, n)
        return pltpu.make_async_remote_copy(
            src_ref=part_ref.at[pl.ds(to * share, share)],
            dst_ref=got_part.at[step],
            send_sem=part_send.at[step],
            recv_sem=part_recv.at[step],
            device_id={"wide": to},
            device_id_type=MESH,
        )

    for step in range(n - 1, 0, -1):
        part_copy(step).start()
    for copy in tables[1:]:
        copy.wait()
    totals = [part_ref[me * share + sub].astype(F32) for sub in range(share)]
    for step in range(n - 1, 0, -1):
        part_copy(step).wait()
        totals = [t + got_part[step, sub].astype(F32) for sub, t in enumerate(totals)]

    col = lax.broadcasted_iota(jnp.int32, (8, LANES), 1)
    t_c, t_s = cos_sin_turns(((col % 8) * row8).astype(F32) * 0.125)
    mix = jnp.where(col % 16 < 8, t_c, -t_s)[:, :32].astype(BF16)
    for sub in range(share):
        lower, upper = untangle(totals[sub][:8]), untangle(totals[sub][8:])
        zero_bin = jnp.logical_and(row8 == 0, jnp.logical_or(col == 0, col == 8))
        lower = jnp.where(zero_bin, 0.5 * lower, lower)
        bins = jnp.concatenate([lower, upper], axis=1).astype(BF16)
        a = jnp.dot(bins, inv_ref[...], preferred_element_type=F32)
        a_re, a_im = a[:, :window], a[:, window:]
        w_re, w_im = twist_ref[0:8, :], twist_ref[8:16, :]
        b = jnp.concatenate([a_re * w_re - a_im * w_im, a_re * w_im + a_im * w_re], axis=0)
        high = b.astype(BF16)
        low = (b - high.astype(F32)).astype(BF16)
        out = jnp.dot(mix, jnp.concatenate([high, low], axis=0), preferred_element_type=F32)
        out = out * (2.0 / (samples * math.sqrt(channels)))
        per = window // LANES
        for p in range(per):
            out_ref[sub, pl.ds(p, 8, stride=per), :] = out[:, p * LANES : (p + 1) * LANES]


def body(n, filterbank, channel_mask, band_edges, dm_delays):
    beams, local, samples = filterbank.shape
    channels = local * n
    bands = band_edges.shape[0] + 1
    trials = dm_delays.shape[0]
    share = trials // n
    window = samples // NBLK
    blocks = samples // 4 // 64
    halves = 8 // (LANES // trials)
    tab = forward_table(samples)
    inv, twist = inverse_tables(samples)
    x = filterbank.reshape(local, samples)

    dma = pltpu.SemaphoreType.DMA((n,))
    series = pl.pallas_call(
        functools.partial(fused_kernel, n, bands, channels, trials),
        out_shape=jax.ShapeDtypeStruct((share, samples // LANES, LANES), F32),
        in_specs=[HBM] * 7,
        out_specs=VMEM,
        scratch_shapes=[
            pltpu.SMEM(band_edges.shape, jnp.int32),
            pltpu.SMEM(dm_delays.shape, jnp.int32),
            pltpu.VMEM((1, local), jnp.int32),
            pltpu.VMEM((local, samples), x.dtype),
            pltpu.VMEM(tab.shape, BF16),
            pltpu.VMEM(inv.shape, BF16),
            pltpu.VMEM(twist.shape, F32),
            pltpu.VMEM((local, NBLK * LANES), BF16),
            pltpu.VMEM((4, local, LANES), F32),
            pltpu.VMEM((4, local, LANES), F32),
            pltpu.VMEM((blocks * halves, local, LANES), F32),
            pltpu.VMEM((blocks * halves, local, LANES), F32),
            pltpu.VMEM((8, local, window), BF16),
            pltpu.VMEM((8, blocks, 16, local), BF16),
            pltpu.VMEM((local, LANES), F32),
            pltpu.VMEM((NBLK, local, LANES), F32),
            pltpu.VMEM((1, LANES), F32),
            pltpu.VMEM((n, 1, LANES), F32),
            pltpu.VMEM((trials, 16, LANES), BF16),
            pltpu.VMEM((n, share, 16, LANES), BF16),
            pltpu.SemaphoreType.DMA((3,)), pltpu.SemaphoreType.DMA((local // 64,)), pltpu.SemaphoreType.DMA((3,)),
            dma, dma, dma, dma,
        ],
        compiler_params=pltpu.CompilerParams(
            collective_id=0, has_side_effects=True, vmem_limit_bytes=24 << 20
        ),
    )(*[
        pltpu.with_memory_space_constraint(v, pltpu.HBM)
        for v in (
            band_edges, dm_delays, channel_mask.reshape(1, local), x,
            jnp.asarray(tab), jnp.asarray(inv), jnp.asarray(twist),
        )
    ])
    return series.reshape(beams, share, samples)


def solution(mesh):
    return jax.shard_map(
        functools.partial(body, mesh.shape["wide"]),
        mesh=mesh,
        in_specs=(P("beam", "wide", None), P(("beam", "wide")), P(), P()),
        out_specs=P("beam", "wide", None),
        check_vma=False,
    )
```

```python
import functools
import math

import jax
import jax.numpy as jnp
import ml_dtypes
import numpy as np
from jax import lax
from jax.experimental import pallas as pl
from jax.experimental.pallas import tpu as pltpu
from jax.sharding import PartitionSpec as P

NBLK = 8
LANES = 128
PARTS = 4
VMEM = pl.BlockSpec(memory_space=pltpu.VMEM)
HBM = pl.BlockSpec(memory_space=pltpu.HBM)
MESH = pl.DeviceIdType.MESH
F32 = jnp.float32
BF16 = jnp.bfloat16


def turn_coefficients():
    degree = 5
    nodes = np.cos((np.arange(64) + 0.5) * np.pi / 64) * 0.125 + 0.125
    root = np.sqrt(nodes)
    cos_fit = np.polynomial.Chebyshev.fit(nodes, np.cos(2 * np.pi * root), degree, domain=[0, 0.25])
    sin_fit = np.polynomial.Chebyshev.fit(
        nodes, np.sin(2 * np.pi * root) / root, degree, domain=[0, 0.25]
    )
    as_power = lambda fit: [float(np.float32(v)) for v in fit.convert(kind=np.polynomial.Polynomial).coef]
    return as_power(cos_fit), as_power(sin_fit)


COS_COEF, SIN_COEF = turn_coefficients()


def cos_sin_turns(turns):
    r = turns - jnp.floor(turns + 0.5)
    s = r * r
    c = jnp.full_like(s, COS_COEF[-1])
    q = jnp.full_like(s, SIN_COEF[-1])
    for a, b in zip(COS_COEF[-2::-1], SIN_COEF[-2::-1]):
        c = c * s + a
        q = q * s + b
    return c, q * r


def forward_table(samples):
    window = samples // NBLK
    blocks = samples // 4 // 64
    r = np.arange(8)[:, None, None]
    g = 8 * np.arange(blocks)[None, :, None] + (np.arange(8)[None, None, :] ^ r)
    f = 8 * g + r
    angle = (f[..., None] * np.arange(window) % samples) * (2 * np.pi / samples)
    table = np.stack([np.cos(angle), -np.sin(angle)], axis=2)
    return table.reshape(8 * blocks * 16, window).astype(ml_dtypes.bfloat16)


def inverse_tables(samples, gs):
    window = samples // 8
    groups = samples // 32
    row, high, part, low = np.ix_(range(2), range(gs // 16), range(groups // gs), range(8))
    g = (gs * part + 8 * (2 * high + row) + low).reshape(-1)
    t = np.arange(window)
    angle = (g[:, None] * t[None, :] % window) * (2 * np.pi / window)
    c, s = np.cos(angle), np.sin(angle)
    real = np.concatenate([c, s], axis=1).reshape(groups // 8, 8, 2 * window)
    imag = np.concatenate([-s, c], axis=1).reshape(groups // 8, 8, 2 * window)
    first = np.stack([real, imag], axis=1).reshape(2 * groups, 2 * window)
    turn = np.arange(8)[:, None] * t[None, :] * (2 * np.pi / samples)
    twist = np.concatenate([np.cos(turn), np.sin(turn)], axis=0)
    return first.astype(ml_dtypes.bfloat16), twist.astype(np.float32)


def untangle(x):
    row = lax.broadcasted_iota(jnp.int32, x.shape, 0)
    lane = lax.broadcasted_iota(jnp.int32, x.shape, 1)
    for s in (1, 2, 4):
        low_row, low_lane = (row & s) == 0, (lane & s) == 0
        up = pltpu.roll(x, 8 - s, 0)
        right = pltpu.roll(x, s, 1)
        cross = pltpu.roll(pltpu.roll(x, LANES - s, 1), s, 0)
        x = jnp.where(low_row, jnp.where(low_lane, x, up), jnp.where(low_lane, cross, right))
    return x


def fused_kernel(
    n, bands, channels, trials,
    edges_hbm, delays_hbm, mask_hbm, x_hbm, tab_hbm, inv_hbm, twist_hbm,
    out_ref,
    edges_ref, delays_ref, mask_ref, x_ref, tab_ref, inv_ref, twist_ref, sq_ref, rot_c, rot_s, base_c, base_s,
    y_ref, spec_ref, pick_ref, own_power, got_power, part_ref, got_part,
    small_sem, x_sem, table_sem, power_send, power_recv, part_send, part_recv,
):
    local, samples = x_ref.shape
    window = samples // NBLK
    blocks = samples // 4 // 64
    share = out_ref.shape[0]
    some = trials // PARTS
    gs = LANES // some
    supers = 8 * blocks // gs
    near = gs // 8
    assert gs * some == LANES and gs in (16, 32) and 8 * blocks == LANES
    assert n & (n - 1) == 0 and n * share == trials
    assert bands * NBLK <= LANES
    me = lax.axis_index("wide")
    first = me * local

    def wait_all(slots, sem):
        others = slots.at[pl.ds(1, n - 1)]
        pltpu.make_async_copy(others, others, sem).wait()

    flips = []
    while 1 << len(flips) < n:
        bit = 1 << len(flips)
        flips.append(bit - 2 * bit * lax.rem(me // bit, 2))

    def partner(step):
        to = me
        for b, flip in enumerate(flips):
            if step >> b & 1:
                to = to + flip
        return to

    small = [
        pltpu.make_async_copy(src, dst, small_sem.at[i])
        for i, (src, dst) in enumerate(
            [(delays_hbm, delays_ref), (edges_hbm, edges_ref), (mask_hbm, mask_ref)]
        )
    ]
    for copy in small:
        copy.start()
    rows = 64

    def load(i):
        at = pl.ds(pl.multiple_of(i * rows, rows), rows)
        return pltpu.make_async_copy(x_hbm.at[at], x_ref.at[at], x_sem.at[i])

    for i in range(local // rows):
        load(i).start()

    barrier = pltpu.get_barrier_semaphore()
    for step in range(n - 1, 0, -1):
        pl.semaphore_signal(barrier, inc=1, device_id={"wide": partner(step)}, device_id_type=MESH)

    tables = [
        pltpu.make_async_copy(src, dst, table_sem.at[i])
        for i, (src, dst) in enumerate(
            [(tab_hbm, tab_ref), (inv_hbm, inv_ref), (twist_hbm, twist_ref)]
        )
    ]
    for copy in tables:
        copy.start()
    for copy in small:
        copy.wait()

    lane = lax.broadcasted_iota(jnp.int32, (1, LANES), 1)
    delay_rows = []
    for side in range(PARTS):
        row = jnp.zeros((1, LANES), F32)
        for d in range(some):
            row = jnp.where(lane // gs == d, delays_ref[side * some + d].astype(F32), row)
        delay_rows.append(row * (1.0 / samples))
    offset_row = (lane % gs).astype(F32) * 8.0 + 3.5
    prow = 32

    def phases(i, carry):
        at = pl.ds(pl.multiple_of(i * prow, prow), prow)
        channel = first + i * prow + lax.broadcasted_iota(jnp.int32, (prow, LANES), 0)
        ratio = 0.5 + 0.5 * (channel.astype(F32) + 0.5) / channels
        fraction = (1.0 / (ratio * ratio) - 1.0) / 3.0
        for side, delay_row in enumerate(delay_rows):
            sweep = fraction * delay_row
            half_c, half_s = cos_sin_turns(sweep * 0.5)
            twice = 4.0 * half_c * half_c - 2.0
            before, now = (half_c, -half_s), (half_c, half_s)
            for k in range(4):
                if k:
                    before, now = now, tuple(twice * v - u for u, v in zip(before, now))
                rot_c[4 * side + k, at, :] = now[0]
                rot_s[4 * side + k, at, :] = now[1]
            step_c, step_s = cos_sin_turns(sweep * (8.0 * gs))
            a, b = cos_sin_turns(sweep * offset_row)
            old = (a * step_c + b * step_s, b * step_c - a * step_s)
            now = (a, b)
            double = step_c + step_c
            for k in range(supers):
                base_c[side * supers + k, at, :] = now[0].astype(BF16)
                base_s[side * supers + k, at, :] = now[1].astype(BF16)
                old, now = now, tuple(double * v - u for u, v in zip(old, now))
        return carry

    def square(i, carry):
        load(i).wait()
        at = pl.ds(pl.multiple_of(i * rows, rows), rows)
        for k in range(NBLK):
            total = None
            for p in range(window // LANES):
                v = x_ref[at, pl.ds(k * window + p * LANES, LANES)].astype(F32)
                total = v * v if total is None else total + v * v
            sq_ref[at, pl.ds(k * LANES, LANES)] = total.astype(BF16)
        return carry

    lax.fori_loop(0, local // rows, square, 0)
    channel_row = first + lax.broadcasted_iota(jnp.int32, (1, local), 1)
    keep = mask_ref[...].astype(F32)
    picks = []
    for j in range(bands):
        inside = channel_row < (channels if j == bands - 1 else edges_ref[j])
        if j:
            inside = jnp.logical_and(inside, channel_row >= edges_ref[j - 1])
        picks.append(jnp.where(inside, keep, 0.0))
    pick = jnp.concatenate(picks, axis=0).astype(BF16)
    summed = jnp.dot(pick, sq_ref[...], preferred_element_type=F32)
    spot = lax.broadcasted_iota(jnp.int32, (bands, LANES), 1)
    band_row = lax.broadcasted_iota(jnp.int32, (bands, LANES), 0)
    powers = jnp.zeros((bands, LANES), F32)
    for k in range(NBLK):
        part = jnp.sum(summed[:, k * LANES : (k + 1) * LANES], axis=1, keepdims=True)
        powers = jnp.where(spot == band_row * NBLK + k, part, powers)
    own_power[...] = jnp.sum(powers, axis=0, keepdims=True) * (1.0 / window)

    pl.semaphore_wait(barrier, n - 1)
    for step in range(n - 1, 0, -1):
        pltpu.make_async_remote_copy(
            src_ref=own_power,
            dst_ref=got_power.at[step],
            send_sem=power_send,
            recv_sem=power_recv,
            device_id={"wide": partner(step)},
            device_id_type=MESH,
        ).start()

    lax.fori_loop(0, local // prow, phases, 0)
    pick_ref[...] = jnp.transpose(jnp.broadcast_to(keep, (LANES, local)))
    tables[0].wait()

    total = own_power[...]
    wait_all(got_power, power_recv)
    for step in range(n - 1, 0, -1):
        total = total + got_power[step]
    width = jnp.zeros((1, LANES), jnp.int32)
    for j in range(bands):
        high = channels if j == bands - 1 else edges_ref[j]
        low = edges_ref[j - 1] if j else 0
        width = jnp.where(lane // NBLK == j, high - low, width)
    width = jnp.maximum(width, 1).astype(F32)
    level = 1.0 / jnp.sqrt(total / width + 1e-05)

    levels = [
        jnp.broadcast_to(pltpu.roll(level, LANES - NBLK * j, 1) if j else level, (8, LANES))
        for j in range(bands)
    ]
    for t in range(local // 8):
        at = slice(8 * t, 8 * t + 8)
        channel = first + 8 * t + lax.broadcasted_iota(jnp.int32, (8, LANES), 0)
        scale = levels[-1]
        for j in range(bands - 2, -1, -1):
            scale = jnp.where(channel < edges_ref[j], levels[j], scale)
        pick_ref[at, :] = scale * pick_ref[at, :]
    crow = 16

    def fold(i, carry):
        at = pl.ds(pl.multiple_of(i * crow, crow), crow)
        scale = pick_ref[at, :]
        columns = [jnp.broadcast_to(scale[:, m : m + 1], (crow, LANES)) for m in range(8)]
        root = math.sqrt(0.5)
        for p in range(window // LANES):
            here = slice(p * LANES, (p + 1) * LANES)
            x = [
                x_ref[at, m * window + p * LANES : m * window + (p + 1) * LANES].astype(F32)
                * columns[m]
                for m in range(8)
            ]
            plus = [x[m] + x[m + 4] for m in range(4)]
            minus = [x[m] - x[m + 4] for m in range(4)]
            even, odd = plus[0] + plus[2], plus[1] + plus[3]
            near, far = root * (minus[1] - minus[3]), root * (minus[1] + minus[3])
            folded = (
                even + odd, even - odd,
                minus[0] + near, -(far + minus[2]),
                plus[0] - plus[2], plus[3] - plus[1],
                minus[0] - near, minus[2] - far,
            )
            for k, value in enumerate(folded):
                y_ref[k, at, here] = value.astype(BF16)
        return carry

    lax.fori_loop(0, local // crow, fold, 0, unroll=True)

    def product(which, r):
        both = lax.dot_general(
            tab_ref[r * 16 * blocks : (r + 1) * 16 * blocks, :], y_ref[which],
            (((1,), (1,)), ((), ())), preferred_element_type=F32,
        ).reshape(blocks, 2, 8, local)
        return both[:, 0], both[:, 1]

    for r in range(8):
        if r % 4 == 0:
            re, im = product(r // 4, r)
        else:
            kind = min(r, 8 - r)
            (a_re, a_im), (b_re, b_im) = product(2 * kind, r), product(2 * kind + 1, r)
            if r < 4:
                re, im = a_re - b_im, a_im + b_re
            else:
                re, im = a_re + b_im, a_im - b_re
        spec_ref[r] = jnp.concatenate([re, im], axis=1).astype(BF16)

    row8 = lax.broadcasted_iota(jnp.int32, (8, LANES), 0)
    lane8 = lax.broadcasted_iota(jnp.int32, (8, LANES), 1) % gs
    code = (row8 ^ (lane8 % 8)) + lane8 // 8 * 8
    fourth = n // PARTS
    corner = lax.rem(me, fourth)
    bits = [lax.rem(me // (fourth << b), 2) for b in range(PARTS.bit_length() - 1)]

    def part_copy(step, to):
        return pltpu.make_async_remote_copy(
            src_ref=part_ref.at[pl.ds(to * share, share)],
            dst_ref=got_part.at[step],
            send_sem=part_send,
            recv_sem=part_recv,
            device_id={"wide": to},
            device_id_type=MESH,
        )

    for side in range(PARTS):
        kept = []
        for block in range(supers):
            xa, xb = base_c[side * supers + block], base_s[side * supers + block]
            got_re = got_im = jnp.zeros((8, LANES), F32)
            for k in range(4):
                c, s = rot_c[4 * side + k].astype(BF16), rot_s[4 * side + k].astype(BF16)
                moving = jnp.concatenate(
                    [spec_ref[j, near * block + q] for j in (3 - k, 4 + k) for q in range(near)], axis=0
                )
                one = jnp.concatenate([c * xa, s * xb], axis=1)
                two = jnp.concatenate([s * xa, c * xb], axis=1)
                one = jnp.dot(moving, one, preferred_element_type=F32)
                two = jnp.dot(moving, two, preferred_element_type=F32)
                ac, bs, as_, bc = one[:, :LANES], one[:, LANES:], two[:, :LANES], two[:, LANES:]
                for q in range(near):
                    re = slice(16 * q, 16 * q + 8)
                    im = slice(16 * q + 8, 16 * q + 16)
                    out_re = (ac[re] + bs[re]) - (bc[im] - as_[im])
                    out_im = (bc[re] - as_[re]) + (ac[im] + bs[im])
                    got_re = jnp.where(code == 8 * q + 3 - k, out_re, got_re)
                    got_im = jnp.where(code == 8 * q + 3 - k, out_im, got_im)
                    re = slice(16 * (near + q), 16 * (near + q) + 8)
                    im = slice(16 * (near + q) + 8, 16 * (near + q) + 16)
                    out_re = (ac[re] - bs[re]) - (as_[im] + bc[im])
                    out_im = (as_[re] + bc[re]) + (ac[im] - bs[im])
                    got_re = jnp.where(code == 8 * q + 4 + k, out_re, got_re)
                    got_im = jnp.where(code == 8 * q + 4 + k, out_im, got_im)
            kept.append(jnp.concatenate([got_re, got_im], axis=0))
        turned = jnp.transpose(jnp.concatenate(kept, axis=0))
        for d in range(some):
            pieces = [turned[u : u + 16] for u in range(d * gs, (d + 1) * gs, 16)]
            part_ref[side * some + d] = jnp.concatenate(pieces, axis=1).astype(BF16)
        flipped = [1 - v if side >> b & 1 else v for b, v in enumerate(bits)]
        base = sum(v * (fourth << b) for b, v in enumerate(flipped))
        for i in range(fourth - 1, 0, -1):
            to = side * fourth + corner
            for b, flip in enumerate(flips):
                if i >> b & 1:
                    to = to + flip
            part_copy(base + i, to).start()

        @pl.when(base > 0)
        def _():
            part_copy(base, side * fourth + corner).start()

    col = lax.broadcasted_iota(jnp.int32, (8, LANES), 1)
    t_c, t_s = cos_sin_turns(((col % 8) * row8).astype(F32) * 0.125)
    mix = jnp.where(col % 16 < 8, t_c, -t_s)[:, :32].astype(BF16)
    for copy in tables[1:]:
        copy.wait()
    totals = [part_ref[me * share + sub].astype(F32) for sub in range(share)]
    wait_all(got_part, part_recv)
    for step in range(n - 1, 0, -1):
        totals = [t + got_part[step, sub].astype(F32) for sub, t in enumerate(totals)]

    for sub in range(share):
        lower, upper = untangle(totals[sub][:8]), untangle(totals[sub][8:])
        zero_bin = jnp.logical_and(row8 == 0, jnp.logical_or(col == 0, col == 8))
        lower = jnp.where(zero_bin, 0.5 * lower, lower)
        bins = jnp.concatenate([lower, upper], axis=1).astype(BF16)
        a = jnp.dot(bins, inv_ref[...], preferred_element_type=F32)
        a_re, a_im = a[:, :window], a[:, window:]
        w_re, w_im = twist_ref[0:8, :], twist_ref[8:16, :]
        b = jnp.concatenate([a_re * w_re - a_im * w_im, a_re * w_im + a_im * w_re], axis=0)
        high = b.astype(BF16)
        low = (b - high.astype(F32)).astype(BF16)
        out = jnp.dot(mix, jnp.concatenate([high, low], axis=0), preferred_element_type=F32)
        out = out * (2.0 / (samples * math.sqrt(channels)))
        per = window // LANES
        for p in range(per):
            out_ref[sub, pl.ds(p, 8, stride=per), :] = out[:, p * LANES : (p + 1) * LANES]
    wait_all(got_power, power_send)
    wait_all(got_part, part_send)


def body(n, filterbank, channel_mask, band_edges, dm_delays):
    beams, local, samples = filterbank.shape
    channels = local * n
    bands = band_edges.shape[0] + 1
    trials = dm_delays.shape[0]
    share = trials // n
    window = samples // NBLK
    gs = PARTS * LANES // trials
    supers = samples // 32 // gs
    tab = forward_table(samples)
    inv, twist = inverse_tables(samples, gs)
    x = filterbank.reshape(local, samples)

    dma = pltpu.SemaphoreType.DMA
    series = pl.pallas_call(
        functools.partial(fused_kernel, n, bands, channels, trials),
        out_shape=jax.ShapeDtypeStruct((share, samples // LANES, LANES), F32),
        in_specs=[HBM] * 7,
        out_specs=VMEM,
        scratch_shapes=[
            pltpu.SMEM(band_edges.shape, jnp.int32),
            pltpu.SMEM(dm_delays.shape, jnp.int32),
            pltpu.VMEM((1, local), jnp.int32),
            pltpu.VMEM((local, samples), x.dtype),
            pltpu.VMEM(tab.shape, BF16),
            pltpu.VMEM(inv.shape, BF16),
            pltpu.VMEM(twist.shape, F32),
            pltpu.VMEM((local, NBLK * LANES), BF16),
            pltpu.VMEM((4 * PARTS, local, LANES), F32),
            pltpu.VMEM((4 * PARTS, local, LANES), F32),
            pltpu.VMEM((PARTS * supers, local, LANES), BF16),
            pltpu.VMEM((PARTS * supers, local, LANES), BF16),
            pltpu.VMEM((8, local, window), BF16),
            pltpu.VMEM((8, samples // 256, 16, local), BF16),
            pltpu.VMEM((local, LANES), F32),
            pltpu.VMEM((1, LANES), F32),
            pltpu.VMEM((n, 1, LANES), F32),
            pltpu.VMEM((trials, 16, LANES), BF16),
            pltpu.VMEM((n, share, 16, LANES), BF16),
            pltpu.SemaphoreType.DMA((3,)), pltpu.SemaphoreType.DMA((local // 64,)), pltpu.SemaphoreType.DMA((3,)),
            dma, dma, dma, dma,
        ],
        compiler_params=pltpu.CompilerParams(
            collective_id=0, has_side_effects=True, vmem_limit_bytes=24 << 20
        ),
    )(*[
        pltpu.with_memory_space_constraint(v, pltpu.HBM)
        for v in (
            band_edges, dm_delays, channel_mask.reshape(1, local), x,
            jnp.asarray(tab), jnp.asarray(inv), jnp.asarray(twist),
        )
    ])
    return series.reshape(beams, share, samples)


def solution(mesh):
    return jax.shard_map(
        functools.partial(body, mesh.shape["wide"]),
        mesh=mesh,
        in_specs=(P("beam", "wide", None), P(("beam", "wide")), P(), P()),
        out_specs=P("beam", "wide", None),
        check_vma=False,
    )
```

```python
import functools
import math

import jax
import jax.numpy as jnp
import ml_dtypes
import numpy as np
from jax import lax
from jax.experimental import pallas as pl
from jax.experimental.pallas import tpu as pltpu
from jax.sharding import PartitionSpec as P

NBLK = 8
LANES = 128
PARTS = 4
ORDER = (0, 4, 1, 7, 2, 6, 3, 5)
VMEM = pl.BlockSpec(memory_space=pltpu.VMEM)
HBM = pl.BlockSpec(memory_space=pltpu.HBM)
MESH = pl.DeviceIdType.MESH
F32 = jnp.float32
BF16 = jnp.bfloat16


def turn_coefficients():
    degree = 5
    nodes = np.cos((np.arange(64) + 0.5) * np.pi / 64) * 0.125 + 0.125
    root = np.sqrt(nodes)
    cos_fit = np.polynomial.Chebyshev.fit(nodes, np.cos(2 * np.pi * root), degree, domain=[0, 0.25])
    sin_fit = np.polynomial.Chebyshev.fit(
        nodes, np.sin(2 * np.pi * root) / root, degree, domain=[0, 0.25]
    )
    as_power = lambda fit: [float(np.float32(v)) for v in fit.convert(kind=np.polynomial.Polynomial).coef]
    return as_power(cos_fit), as_power(sin_fit)


COS_COEF, SIN_COEF = turn_coefficients()


def cos_sin_turns(turns):
    r = turns - jnp.floor(turns + 0.5)
    s = r * r
    c = jnp.full_like(s, COS_COEF[-1])
    q = jnp.full_like(s, SIN_COEF[-1])
    for a, b in zip(COS_COEF[-2::-1], SIN_COEF[-2::-1]):
        c = c * s + a
        q = q * s + b
    return c, q * r


def forward_table(samples):
    window = samples // NBLK
    blocks = samples // 4 // 64
    r = np.array(ORDER)[:, None, None]
    g = 8 * np.arange(blocks)[None, :, None] + (np.arange(8)[None, None, :] ^ r)
    f = 8 * g + r
    angle = (f[..., None] * np.arange(window) % samples) * (2 * np.pi / samples)
    table = np.stack([np.cos(angle), -np.sin(angle)], axis=2)
    return table.reshape(8 * blocks * 16, window).astype(ml_dtypes.bfloat16)


def inverse_tables(samples, gs):
    window = samples // 8
    groups = samples // 32
    row, high, part, low = np.ix_(range(2), range(gs // 16), range(groups // gs), range(8))
    g = (gs * part + 8 * (2 * high + row) + low).reshape(-1)
    t = np.arange(window)
    angle = (g[:, None] * t[None, :] % window) * (2 * np.pi / window)
    c, s = np.cos(angle), np.sin(angle)
    real = np.concatenate([c, s], axis=1).reshape(groups // 8, 8, 2 * window)
    imag = np.concatenate([-s, c], axis=1).reshape(groups // 8, 8, 2 * window)
    first = np.stack([real, imag], axis=1).reshape(2 * groups, 2 * window)
    turn = np.arange(8)[:, None] * t[None, :] * (2 * np.pi / samples)
    twist = np.concatenate([np.cos(turn), np.sin(turn)], axis=0)
    return first.astype(ml_dtypes.bfloat16), twist.astype(np.float32)


def untangle(x):
    row = lax.broadcasted_iota(jnp.int32, x.shape, 0)
    lane = lax.broadcasted_iota(jnp.int32, x.shape, 1)
    for s in (1, 2, 4):
        low_row, low_lane = (row & s) == 0, (lane & s) == 0
        up = pltpu.roll(x, 8 - s, 0)
        right = pltpu.roll(x, s, 1)
        cross = pltpu.roll(pltpu.roll(x, LANES - s, 1), s, 0)
        x = jnp.where(low_row, jnp.where(low_lane, x, up), jnp.where(low_lane, cross, right))
    return x


def fused_kernel(
    n, bands, channels, trials,
    edges_hbm, delays_hbm, mask_hbm, x_hbm, tab_hbm, inv_hbm, twist_hbm,
    out_ref,
    edges_ref, delays_ref, mask_ref, x_ref, tab_ref, inv_ref, twist_ref, sq_ref, rot_c, rot_s, base_c, base_s,
    y_ref, minus_ref, spec_ref, pick_ref, own_power, got_power, part_ref, got_part,
    small_sem, x_sem, send_sem, power_recv, part_recv,
):
    local, samples = x_ref.shape
    window = samples // NBLK
    blocks = samples // 4 // 64
    share = out_ref.shape[0]
    some = trials // PARTS
    gs = LANES // some
    supers = 8 * blocks // gs
    near = gs // 8
    assert gs * some == LANES and gs in (16, 32) and 8 * blocks == LANES
    assert n & (n - 1) == 0 and n * share == trials
    assert bands * NBLK <= LANES
    me = lax.axis_index("wide")
    first = me * local

    def wait_all(slots, sem):
        others = slots.at[pl.ds(1, n - 1)]
        pltpu.make_async_copy(others, others, sem).wait()

    flips = []
    while 1 << len(flips) < n:
        bit = 1 << len(flips)
        flips.append(bit - 2 * bit * lax.rem(me // bit, 2))

    def partner(step):
        to = me
        for b, flip in enumerate(flips):
            if step >> b & 1:
                to = to + flip
        return to

    small = [
        pltpu.make_async_copy(src, dst, small_sem.at[i])
        for i, (src, dst) in enumerate(
            [(delays_hbm, delays_ref), (edges_hbm, edges_ref), (mask_hbm, mask_ref)]
        )
    ]
    for copy in small:
        copy.start()
    rows = 64

    whole = pltpu.make_async_copy(x_hbm, x_ref, x_sem)
    whole.start()

    barrier = pltpu.get_barrier_semaphore()
    for step in range(n - 1, 0, -1):
        pl.semaphore_signal(barrier, inc=1, device_id={"wide": partner(step)}, device_id_type=MESH)

    tables = [
        pltpu.make_async_copy(src, dst, small_sem.at[i])
        for i, (src, dst) in enumerate(
            [(tab_hbm, tab_ref), (inv_hbm, inv_ref), (twist_hbm, twist_ref)]
        )
    ]
    for copy in small:
        copy.wait()
    for copy in tables:
        copy.start()

    lane = lax.broadcasted_iota(jnp.int32, (1, LANES), 1)
    delay_rows = []
    for side in range(PARTS):
        row = jnp.zeros((1, LANES), F32)
        for d in range(some):
            row = jnp.where(lane // gs == d, delays_ref[side * some + d].astype(F32), row)
        delay_rows.append(row * (1.0 / samples))
    offset_row = (lane % gs).astype(F32) * 8.0 + 3.5
    prow = 32

    def phases(i, carry):
        at = pl.ds(pl.multiple_of(i * prow, prow), prow)
        channel = first + i * prow + lax.broadcasted_iota(jnp.int32, (prow, LANES), 0)
        ratio = 0.5 + 0.5 * (channel.astype(F32) + 0.5) / channels
        fraction = (1.0 / (ratio * ratio) - 1.0) / 3.0
        for side, delay_row in enumerate(delay_rows):
            sweep = fraction * delay_row
            half_c, half_s = cos_sin_turns(sweep * 0.5)
            twice = 4.0 * half_c * half_c - 2.0
            before, now = (half_c, -half_s), (half_c, half_s)
            for k in range(4):
                if k:
                    before, now = now, tuple(twice * v - u for u, v in zip(before, now))
                rot_c[4 * side + k, at, :] = now[0]
                rot_s[4 * side + k, at, :] = now[1]
            step_c, step_s = cos_sin_turns(sweep * (8.0 * gs))
            a, b = cos_sin_turns(sweep * offset_row)
            old = (a * step_c + b * step_s, b * step_c - a * step_s)
            now = (a, b)
            double = step_c + step_c
            for k in range(supers):
                base_c[side * supers + k, at, :] = now[0].astype(BF16)
                base_s[side * supers + k, at, :] = now[1].astype(BF16)
                old, now = now, tuple(double * v - u for u, v in zip(old, now))
        return carry

    def square(i, carry):
        at = pl.ds(pl.multiple_of(i * rows, rows), rows)
        for k in range(NBLK):
            total = None
            for p in range(window // LANES):
                v = x_ref[at, pl.ds(k * window + p * LANES, LANES)].astype(F32)
                total = v * v if total is None else total + v * v
            sq_ref[at, pl.ds(k * LANES, LANES)] = total.astype(BF16)
        return carry

    whole.wait()
    lax.fori_loop(0, local // rows, square, 0)
    channel_row = first + lax.broadcasted_iota(jnp.int32, (1, local), 1)
    keep = mask_ref[...].astype(F32)
    picks = []
    for j in range(bands):
        inside = channel_row < (channels if j == bands - 1 else edges_ref[j])
        if j:
            inside = jnp.logical_and(inside, channel_row >= edges_ref[j - 1])
        picks.append(jnp.where(inside, keep, 0.0))
    pick = jnp.concatenate(picks, axis=0).astype(BF16)
    summed = jnp.dot(pick, sq_ref[...], preferred_element_type=F32)
    spot = lax.broadcasted_iota(jnp.int32, (bands, LANES), 1)
    band_row = lax.broadcasted_iota(jnp.int32, (bands, LANES), 0)
    powers = jnp.zeros((bands, LANES), F32)
    for k in range(NBLK):
        part = jnp.sum(summed[:, k * LANES : (k + 1) * LANES], axis=1, keepdims=True)
        powers = jnp.where(spot == band_row * NBLK + k, part, powers)
    own_power[...] = jnp.sum(powers, axis=0, keepdims=True) * (1.0 / window)

    pl.semaphore_wait(barrier, n - 1)
    for step in range(n - 1, 0, -1):
        pltpu.make_async_remote_copy(
            src_ref=own_power,
            dst_ref=got_power.at[step],
            send_sem=send_sem,
            recv_sem=power_recv,
            device_id={"wide": partner(step)},
            device_id_type=MESH,
        ).start()

    lax.fori_loop(0, local // prow, phases, 0)
    pick_ref[...] = jnp.transpose(jnp.broadcast_to(keep, (LANES, local)))
    tables[0].wait()

    total = own_power[...]
    wait_all(got_power, send_sem)
    wait_all(got_power, power_recv)
    for step in range(n - 1, 0, -1):
        total = total + got_power[step]
    width = jnp.zeros((1, LANES), jnp.int32)
    for j in range(bands):
        high = channels if j == bands - 1 else edges_ref[j]
        low = edges_ref[j - 1] if j else 0
        width = jnp.where(lane // NBLK == j, high - low, width)
    width = jnp.maximum(width, 1).astype(F32)
    level = 1.0 / jnp.sqrt(total / width + 1e-05)

    levels = [
        jnp.broadcast_to(pltpu.roll(level, LANES - NBLK * j, 1) if j else level, (8, LANES))
        for j in range(bands)
    ]
    for t in range(local // 8):
        at = slice(8 * t, 8 * t + 8)
        channel = first + 8 * t + lax.broadcasted_iota(jnp.int32, (8, LANES), 0)
        scale = levels[-1]
        for j in range(bands - 2, -1, -1):
            scale = jnp.where(channel < edges_ref[j], levels[j], scale)
        pick_ref[at, :] = scale * pick_ref[at, :]
    crow = 16

    def fold(at):
        scale = pick_ref[at, :]
        columns = [jnp.broadcast_to(scale[:, m : m + 1], (crow, LANES)) for m in range(8)]
        for p in range(window // LANES):
            here = slice(p * LANES, (p + 1) * LANES)
            x = [
                x_ref[at, m * window + p * LANES : m * window + (p + 1) * LANES].astype(F32)
                * columns[m]
                for m in range(8)
            ]
            plus = [x[m] + x[m + 4] for m in range(4)]
            minus = [x[m] - x[m + 4] for m in range(4)]
            even, odd = plus[0] + plus[2], plus[1] + plus[3]
            folded = (
                (0, even + odd), (1, even - odd), (4, plus[0] - plus[2]), (5, plus[3] - plus[1]),
            )
            for k, value in folded:
                y_ref[k, at, here] = value.astype(BF16)
            for k in range(4):
                minus_ref[k, at, here] = minus[k]

    for i in range(local // crow):
        fold(slice(i * crow, (i + 1) * crow))

    def fold_rest(at):
        root = math.sqrt(0.5)
        for p in range(window // LANES):
            here = slice(p * LANES, (p + 1) * LANES)
            minus = [minus_ref[k, at, here] for k in range(4)]
            near, far = root * (minus[1] - minus[3]), root * (minus[1] + minus[3])
            folded = (
                (2, minus[0] + near), (3, -(far + minus[2])),
                (6, minus[0] - near), (7, minus[2] - far),
            )
            for k, value in folded:
                y_ref[k, at, here] = value.astype(BF16)


    def product(which, first_row, count):
        size = 16 * blocks
        both = lax.dot_general(
            tab_ref[first_row * size : (first_row + count) * size, :], y_ref[which],
            (((1,), (1,)), ((), ())), preferred_element_type=F32,
        ).reshape(count, blocks, 2, 8, local)
        return both[:, :, 0], both[:, :, 1]

    def keep_spectrum(r, re, im):
        spec_ref[r] = jnp.concatenate([re, im], axis=1).astype(BF16)

    for which in range(2):
        re, im = product(which, which, 1)
        keep_spectrum(ORDER[which], re[0], im[0])
    for kind in (2, 1, 3):
        if kind == 1:
            for i in range(local // crow):
                fold_rest(slice(i * crow, (i + 1) * crow))
        (a_re, a_im), (b_re, b_im) = product(2 * kind, 2 * kind, 2), product(2 * kind + 1, 2 * kind, 2)
        keep_spectrum(kind, a_re[0] - b_im[0], a_im[0] + b_re[0])
        keep_spectrum(8 - kind, a_re[1] + b_im[1], a_im[1] - b_re[1])

    row8 = lax.broadcasted_iota(jnp.int32, (8, LANES), 0)
    lane8 = lax.broadcasted_iota(jnp.int32, (8, LANES), 1) % gs
    code = (row8 ^ (lane8 % 8)) + lane8 // 8 * 8
    fourth = n // PARTS
    low_bits = [lax.rem(me // (1 << b), 2) for b in range(fourth.bit_length() - 1)]
    bits = [lax.rem(me // (fourth << b), 2) for b in range(PARTS.bit_length() - 1)]

    def part_copy(step, to):
        return pltpu.make_async_remote_copy(
            src_ref=part_ref.at[pl.ds(to * share, share)],
            dst_ref=got_part.at[step],
            send_sem=send_sem,
            recv_sem=part_recv,
            device_id={"wide": to},
            device_id_type=MESH,
        )

    for side in range(PARTS):
        kept = []
        for block in range(supers):
            xa, xb = base_c[side * supers + block], base_s[side * supers + block]
            got_re = got_im = jnp.zeros((8, LANES), F32)
            for k in range(4):
                c, s = rot_c[4 * side + k].astype(BF16), rot_s[4 * side + k].astype(BF16)
                moving = jnp.concatenate(
                    [spec_ref[j, near * block + q] for j in (3 - k, 4 + k) for q in range(near)], axis=0
                )
                one = jnp.concatenate([c * xa, s * xb], axis=1)
                two = jnp.concatenate([s * xa, c * xb], axis=1)
                one = jnp.dot(moving, one, preferred_element_type=F32)
                two = jnp.dot(moving, two, preferred_element_type=F32)
                ac, bs, as_, bc = one[:, :LANES], one[:, LANES:], two[:, :LANES], two[:, LANES:]
                for q in range(near):
                    re = slice(16 * q, 16 * q + 8)
                    im = slice(16 * q + 8, 16 * q + 16)
                    out_re = (ac[re] + bs[re]) - (bc[im] - as_[im])
                    out_im = (bc[re] - as_[re]) + (ac[im] + bs[im])
                    got_re = jnp.where(code == 8 * q + 3 - k, out_re, got_re)
                    got_im = jnp.where(code == 8 * q + 3 - k, out_im, got_im)
                    re = slice(16 * (near + q), 16 * (near + q) + 8)
                    im = slice(16 * (near + q) + 8, 16 * (near + q) + 16)
                    out_re = (ac[re] - bs[re]) - (as_[im] + bc[im])
                    out_im = (as_[re] + bc[re]) + (ac[im] - bs[im])
                    got_re = jnp.where(code == 8 * q + 4 + k, out_re, got_re)
                    got_im = jnp.where(code == 8 * q + 4 + k, out_im, got_im)
            kept.append(jnp.concatenate([got_re, got_im], axis=0))
        turned = jnp.transpose(jnp.concatenate(kept, axis=0))
        for d in range(some):
            pieces = [turned[u : u + 16] for u in range(d * gs, (d + 1) * gs, 16)]
            part_ref[side * some + d] = jnp.concatenate(pieces, axis=1).astype(BF16)
        flipped = [1 - v if side >> b & 1 else v for b, v in enumerate(bits)]
        base = sum(v * (fourth << b) for b, v in enumerate(flipped))
        for i in range(fourth):
            to = side * fourth + i
            slot = base
            for b, v in enumerate(low_bits):
                slot = slot + ((1 - v if i >> b & 1 else v) << b)

            @pl.when(to != me)
            def _():
                part_copy(slot, to).start()

    col = lax.broadcasted_iota(jnp.int32, (8, LANES), 1)
    t_c, t_s = cos_sin_turns(((col % 8) * row8).astype(F32) * 0.125)
    mix = jnp.where(col % 16 < 8, t_c, -t_s)[:, :32].astype(BF16)
    for copy in tables[1:]:
        copy.wait()
    totals = [part_ref[me * share + sub].astype(F32) for sub in range(share)]
    wait_all(got_part, part_recv)
    for step in range(n - 1, 0, -1):
        totals = [t + got_part[step, sub].astype(F32) for sub, t in enumerate(totals)]

    for sub in range(share):
        lower, upper = untangle(totals[sub][:8]), untangle(totals[sub][8:])
        zero_bin = jnp.logical_and(row8 == 0, jnp.logical_or(col == 0, col == 8))
        lower = jnp.where(zero_bin, 0.5 * lower, lower)
        bins = jnp.concatenate([lower, upper], axis=1).astype(BF16)
        a = jnp.dot(bins, inv_ref[...], preferred_element_type=F32)
        a_re, a_im = a[:, :window], a[:, window:]
        w_re, w_im = twist_ref[0:8, :], twist_ref[8:16, :]
        b = jnp.concatenate([a_re * w_re - a_im * w_im, a_re * w_im + a_im * w_re], axis=0)
        high = b.astype(BF16)
        low = (b - high.astype(F32)).astype(BF16)
        out = jnp.dot(mix, jnp.concatenate([high, low], axis=0), preferred_element_type=F32)
        out = out * (2.0 / (samples * math.sqrt(channels)))
        per = window // LANES
        for p in range(per):
            out_ref[sub, pl.ds(p, 8, stride=per), :] = out[:, p * LANES : (p + 1) * LANES]
    wait_all(got_part, send_sem)


def body(n, filterbank, channel_mask, band_edges, dm_delays):
    beams, local, samples = filterbank.shape
    channels = local * n
    bands = band_edges.shape[0] + 1
    trials = dm_delays.shape[0]
    share = trials // n
    window = samples // NBLK
    gs = PARTS * LANES // trials
    supers = samples // 32 // gs
    tab = forward_table(samples)
    inv, twist = inverse_tables(samples, gs)
    x = filterbank.reshape(local, samples)

    dma = pltpu.SemaphoreType.DMA
    series = pl.pallas_call(
        functools.partial(fused_kernel, n, bands, channels, trials),
        out_shape=jax.ShapeDtypeStruct((share, samples // LANES, LANES), F32),
        in_specs=[HBM] * 7,
        out_specs=VMEM,
        scratch_shapes=[
            pltpu.SMEM(band_edges.shape, jnp.int32),
            pltpu.SMEM(dm_delays.shape, jnp.int32),
            pltpu.VMEM((1, local), jnp.int32),
            pltpu.VMEM((local, samples), x.dtype),
            pltpu.VMEM(tab.shape, BF16),
            pltpu.VMEM(inv.shape, BF16),
            pltpu.VMEM(twist.shape, F32),
            pltpu.VMEM((local, NBLK * LANES), BF16),
            pltpu.VMEM((4 * PARTS, local, LANES), F32),
            pltpu.VMEM((4 * PARTS, local, LANES), F32),
            pltpu.VMEM((PARTS * supers, local, LANES), BF16),
            pltpu.VMEM((PARTS * supers, local, LANES), BF16),
            pltpu.VMEM((8, local, window), BF16),
            pltpu.VMEM((4, local, window), F32),
            pltpu.VMEM((8, samples // 256, 16, local), BF16),
            pltpu.VMEM((local, LANES), F32),
            pltpu.VMEM((1, LANES), F32),
            pltpu.VMEM((n, 1, LANES), F32),
            pltpu.VMEM((trials, 16, LANES), BF16),
            pltpu.VMEM((n, share, 16, LANES), BF16),
            pltpu.SemaphoreType.DMA((3,)), dma, dma, dma, dma,
        ],
        compiler_params=pltpu.CompilerParams(
            collective_id=0, has_side_effects=True, vmem_limit_bytes=24 << 20
        ),
    )(*[
        pltpu.with_memory_space_constraint(v, pltpu.HBM)
        for v in (
            band_edges, dm_delays, channel_mask.reshape(1, local), x,
            jnp.asarray(tab), jnp.asarray(inv), jnp.asarray(twist),
        )
    ])
    return series.reshape(beams, share, samples)


def solution(mesh):
    return jax.shard_map(
        functools.partial(body, mesh.shape["wide"]),
        mesh=mesh,
        in_specs=(P("beam", "wide", None), P(("beam", "wide")), P(), P()),
        out_specs=P("beam", "wide", None),
        check_vma=False,
    )
```

```python
import functools
import math

import jax
import jax.numpy as jnp
import ml_dtypes
import numpy as np
from jax import lax
from jax.experimental import pallas as pl
from jax.experimental.pallas import tpu as pltpu
from jax.sharding import PartitionSpec as P

NBLK = 8
LANES = 128
PARTS = 4
ORDER = (0, 4, 1, 7, 2, 6, 3, 5)
VMEM = pl.BlockSpec(memory_space=pltpu.VMEM)
HBM = pl.BlockSpec(memory_space=pltpu.HBM)
MESH = pl.DeviceIdType.MESH
F32 = jnp.float32
BF16 = jnp.bfloat16


def turn_coefficients():
    degree = 5
    nodes = np.cos((np.arange(64) + 0.5) * np.pi / 64) * 0.125 + 0.125
    root = np.sqrt(nodes)
    cos_fit = np.polynomial.Chebyshev.fit(nodes, np.cos(2 * np.pi * root), degree, domain=[0, 0.25])
    sin_fit = np.polynomial.Chebyshev.fit(
        nodes, np.sin(2 * np.pi * root) / root, degree, domain=[0, 0.25]
    )
    as_power = lambda fit: [float(np.float32(v)) for v in fit.convert(kind=np.polynomial.Polynomial).coef]
    return as_power(cos_fit), as_power(sin_fit)


COS_COEF, SIN_COEF = turn_coefficients()


def cos_sin_turns(turns):
    r = turns - jnp.floor(turns + 0.5)
    s = r * r
    c = jnp.full_like(s, COS_COEF[-1])
    q = jnp.full_like(s, SIN_COEF[-1])
    for a, b in zip(COS_COEF[-2::-1], SIN_COEF[-2::-1]):
        c = c * s + a
        q = q * s + b
    return c, q * r


def forward_table(samples):
    window = samples // NBLK
    blocks = samples // 4 // 64
    r = np.array(ORDER)[:, None, None]
    g = 8 * np.arange(blocks)[None, :, None] + (np.arange(8)[None, None, :] ^ r)
    f = 8 * g + r
    angle = (f[..., None] * np.arange(window) % samples) * (2 * np.pi / samples)
    table = np.stack([np.cos(angle), -np.sin(angle)], axis=2)
    return table.reshape(8 * blocks * 16, window).astype(ml_dtypes.bfloat16)


def inverse_tables(samples, gs):
    window = samples // 8
    groups = samples // 32
    row, high, part, low = np.ix_(range(2), range(gs // 16), range(groups // gs), range(8))
    g = (gs * part + 8 * (2 * high + row) + low).reshape(-1)
    t = np.arange(window)
    angle = (g[:, None] * t[None, :] % window) * (2 * np.pi / window)
    c, s = np.cos(angle), np.sin(angle)
    real = np.concatenate([c, s], axis=1).reshape(groups // 8, 8, 2 * window)
    imag = np.concatenate([-s, c], axis=1).reshape(groups // 8, 8, 2 * window)
    first = np.stack([real, imag], axis=1).reshape(2 * groups, 2 * window)
    turn = np.arange(8)[:, None] * t[None, :] * (2 * np.pi / samples)
    twist = np.concatenate([np.cos(turn), np.sin(turn)], axis=0)
    return first.astype(ml_dtypes.bfloat16), twist.astype(np.float32)


def untangle(x):
    row = lax.broadcasted_iota(jnp.int32, x.shape, 0)
    lane = lax.broadcasted_iota(jnp.int32, x.shape, 1)
    for s in (1, 2, 4):
        low_row, low_lane = (row & s) == 0, (lane & s) == 0
        up = pltpu.roll(x, 8 - s, 0)
        right = pltpu.roll(x, s, 1)
        cross = pltpu.roll(pltpu.roll(x, LANES - s, 1), s, 0)
        x = jnp.where(low_row, jnp.where(low_lane, x, up), jnp.where(low_lane, cross, right))
    return x


def fused_kernel(
    n, bands, channels, trials,
    edges_hbm, delays_hbm, mask_hbm, x_hbm, tab_hbm, inv_hbm, twist_hbm,
    out_ref,
    edges_ref, delays_ref, mask_ref, x_ref, tab_ref, inv_ref, twist_ref, sq_ref, rot_c, rot_s, base_c, base_s,
    y_ref, minus_ref, spec_ref, pick_ref, own_power, got_power, part_ref, got_part,
    small_sem, x_sem, send_sem, power_recv, part_recv,
):
    local, samples = x_ref.shape
    window = samples // NBLK
    blocks = samples // 4 // 64
    share = out_ref.shape[0]
    some = trials // PARTS
    gs = LANES // some
    supers = 8 * blocks // gs
    near = gs // 8
    assert gs * some == LANES and gs in (16, 32) and 8 * blocks == LANES
    assert n & (n - 1) == 0 and n * share == trials
    assert bands * NBLK <= LANES
    me = lax.axis_index("wide")
    first = me * local

    def wait_all(slots, sem):
        others = slots.at[pl.ds(1, n - 1)]
        pltpu.make_async_copy(others, others, sem).wait()

    flips = []
    while 1 << len(flips) < n:
        bit = 1 << len(flips)
        flips.append(bit - 2 * bit * lax.rem(me // bit, 2))

    def partner(step):
        to = me
        for b, flip in enumerate(flips):
            if step >> b & 1:
                to = to + flip
        return to

    small = [
        pltpu.make_async_copy(src, dst, small_sem.at[i])
        for i, (src, dst) in enumerate(
            [(delays_hbm, delays_ref), (edges_hbm, edges_ref), (mask_hbm, mask_ref)]
        )
    ]
    for copy in small:
        copy.start()
    rows = 64

    whole = pltpu.make_async_copy(x_hbm, x_ref, x_sem)
    whole.start()

    barrier = pltpu.get_barrier_semaphore()
    for step in range(n - 1, 0, -1):
        pl.semaphore_signal(barrier, inc=1, device_id={"wide": partner(step)}, device_id_type=MESH)

    tables = [
        pltpu.make_async_copy(src, dst, small_sem.at[i])
        for i, (src, dst) in enumerate(
            [(tab_hbm, tab_ref), (inv_hbm, inv_ref), (twist_hbm, twist_ref)]
        )
    ]
    for copy in small:
        copy.wait()
    for copy in tables:
        copy.start()

    lane = lax.broadcasted_iota(jnp.int32, (1, LANES), 1)
    delay_rows = []
    for side in range(PARTS):
        row = jnp.zeros((1, LANES), F32)
        for d in range(some):
            row = jnp.where(lane // gs == d, delays_ref[side * some + d].astype(F32), row)
        delay_rows.append(row * (1.0 / samples))
    offset_row = (lane % gs).astype(F32) * 8.0 + 3.5
    prow = 32

    def phases(i, carry):
        at = pl.ds(pl.multiple_of(i * prow, prow), prow)
        channel = first + i * prow + lax.broadcasted_iota(jnp.int32, (prow, LANES), 0)
        ratio = 0.5 + 0.5 * (channel.astype(F32) + 0.5) / channels
        fraction = (1.0 / (ratio * ratio) - 1.0) / 3.0
        for side, delay_row in enumerate(delay_rows):
            sweep = fraction * delay_row
            half_c, half_s = cos_sin_turns(sweep * 0.5)
            twice = 4.0 * half_c * half_c - 2.0
            before, now = (half_c, -half_s), (half_c, half_s)
            for k in range(4):
                if k:
                    before, now = now, tuple(twice * v - u for u, v in zip(before, now))
                rot_c[4 * side + k, at, :] = now[0]
                rot_s[4 * side + k, at, :] = now[1]
            step_c, step_s = cos_sin_turns(sweep * (8.0 * gs))
            a, b = cos_sin_turns(sweep * offset_row)
            old = (a * step_c + b * step_s, b * step_c - a * step_s)
            now = (a, b)
            double = step_c + step_c
            for k in range(supers):
                base_c[side * supers + k, at, :] = now[0].astype(BF16)
                base_s[side * supers + k, at, :] = now[1].astype(BF16)
                old, now = now, tuple(double * v - u for u, v in zip(old, now))
        return carry

    def square(i, carry):
        at = pl.ds(pl.multiple_of(i * rows, rows), rows)
        for k in range(NBLK):
            total = None
            for p in range(window // LANES):
                v = x_ref[at, pl.ds(k * window + p * LANES, LANES)].astype(F32)
                total = v * v if total is None else total + v * v
            sq_ref[at, pl.ds(k * LANES, LANES)] = total.astype(BF16)
        return carry

    whole.wait()
    lax.fori_loop(0, local // rows, square, 0)
    channel_row = first + lax.broadcasted_iota(jnp.int32, (1, local), 1)
    keep = mask_ref[...].astype(F32)
    picks = []
    for j in range(bands):
        inside = channel_row < (channels if j == bands - 1 else edges_ref[j])
        if j:
            inside = jnp.logical_and(inside, channel_row >= edges_ref[j - 1])
        picks.append(jnp.where(inside, keep, 0.0))
    pick = jnp.concatenate(picks, axis=0).astype(BF16)
    summed = jnp.dot(pick, sq_ref[...], preferred_element_type=F32)
    spot = lax.broadcasted_iota(jnp.int32, (bands, LANES), 1)
    band_row = lax.broadcasted_iota(jnp.int32, (bands, LANES), 0)
    powers = jnp.zeros((bands, LANES), F32)
    for k in range(NBLK):
        part = jnp.sum(summed[:, k * LANES : (k + 1) * LANES], axis=1, keepdims=True)
        powers = jnp.where(spot == band_row * NBLK + k, part, powers)
    own_power[...] = jnp.sum(powers, axis=0, keepdims=True) * (1.0 / window)

    pl.semaphore_wait(barrier, n - 1)
    for step in range(n - 1, 0, -1):
        pltpu.make_async_remote_copy(
            src_ref=own_power,
            dst_ref=got_power.at[step],
            send_sem=send_sem,
            recv_sem=power_recv,
            device_id={"wide": partner(step)},
            device_id_type=MESH,
        ).start()

    lax.fori_loop(0, local // prow, phases, 0)
    pick_ref[...] = jnp.transpose(jnp.broadcast_to(keep, (LANES, local)))
    tables[0].wait()

    total = own_power[...]
    wait_all(got_power, send_sem)
    wait_all(got_power, power_recv)
    for step in range(n - 1, 0, -1):
        total = total + got_power[step]
    width = jnp.zeros((1, LANES), jnp.int32)
    for j in range(bands):
        high = channels if j == bands - 1 else edges_ref[j]
        low = edges_ref[j - 1] if j else 0
        width = jnp.where(lane // NBLK == j, high - low, width)
    width = jnp.maximum(width, 1).astype(F32)
    level = 1.0 / jnp.sqrt(total / width + 1e-05)

    levels = [
        jnp.broadcast_to(pltpu.roll(level, LANES - NBLK * j, 1) if j else level, (8, LANES))
        for j in range(bands)
    ]
    for t in range(local // 8):
        at = slice(8 * t, 8 * t + 8)
        channel = first + 8 * t + lax.broadcasted_iota(jnp.int32, (8, LANES), 0)
        scale = levels[-1]
        for j in range(bands - 2, -1, -1):
            scale = jnp.where(channel < edges_ref[j], levels[j], scale)
        pick_ref[at, :] = scale * pick_ref[at, :]
    crow = 16

    def fold(at):
        scale = pick_ref[at, :]
        columns = [jnp.broadcast_to(scale[:, m : m + 1], (crow, LANES)) for m in range(8)]
        for p in range(window // LANES):
            here = slice(p * LANES, (p + 1) * LANES)
            x = [
                x_ref[at, m * window + p * LANES : m * window + (p + 1) * LANES].astype(F32)
                * columns[m]
                for m in range(8)
            ]
            plus = [x[m] + x[m + 4] for m in range(4)]
            minus = [x[m] - x[m + 4] for m in range(4)]
            even, odd = plus[0] + plus[2], plus[1] + plus[3]
            folded = (
                (0, even + odd), (1, even - odd), (4, plus[0] - plus[2]), (5, plus[3] - plus[1]),
            )
            for k, value in folded:
                y_ref[k, at, here] = value.astype(BF16)
            for k in range(4):
                minus_ref[k, at, here] = minus[k]

    for i in range(local // crow):
        fold(slice(i * crow, (i + 1) * crow))

    def fold_rest(at):
        root = math.sqrt(0.5)
        for p in range(window // LANES):
            here = slice(p * LANES, (p + 1) * LANES)
            minus = [minus_ref[k, at, here] for k in range(4)]
            near, far = root * (minus[1] - minus[3]), root * (minus[1] + minus[3])
            folded = (
                (2, minus[0] + near), (3, -(far + minus[2])),
                (6, minus[0] - near), (7, minus[2] - far),
            )
            for k, value in folded:
                y_ref[k, at, here] = value.astype(BF16)


    def product(which, first_row, count):
        size = 16 * blocks
        both = lax.dot_general(
            tab_ref[first_row * size : (first_row + count) * size, :], y_ref[which],
            (((1,), (1,)), ((), ())), preferred_element_type=F32,
        ).reshape(count, blocks, 2, 8, local)
        return both[:, :, 0], both[:, :, 1]

    def keep_spectrum(r, re, im):
        spec_ref[r] = jnp.concatenate([re, im], axis=1).astype(BF16)

    for which in range(2):
        re, im = product(which, which, 1)
        keep_spectrum(ORDER[which], re[0], im[0])
    for kind in (2, 1, 3):
        if kind == 1:
            for i in range(local // crow):
                fold_rest(slice(i * crow, (i + 1) * crow))
        (a_re, a_im), (b_re, b_im) = product(2 * kind, 2 * kind, 2), product(2 * kind + 1, 2 * kind, 2)
        keep_spectrum(kind, a_re[0] - b_im[0], a_im[0] + b_re[0])
        keep_spectrum(8 - kind, a_re[1] + b_im[1], a_im[1] - b_re[1])

    row8 = lax.broadcasted_iota(jnp.int32, (8, LANES), 0)
    lane8 = lax.broadcasted_iota(jnp.int32, (8, LANES), 1) % gs
    code = (row8 ^ (lane8 % 8)) + lane8 // 8 * 8
    fourth = n // PARTS
    low_bits = [lax.rem(me // (1 << b), 2) for b in range(fourth.bit_length() - 1)]
    bits = [lax.rem(me // (fourth << b), 2) for b in range(PARTS.bit_length() - 1)]

    def part_copy(step, to):
        return pltpu.make_async_remote_copy(
            src_ref=part_ref.at[pl.ds(to * share, share)],
            dst_ref=got_part.at[step],
            send_sem=send_sem,
            recv_sem=part_recv,
            device_id={"wide": to},
            device_id_type=MESH,
        )

    for side in range(PARTS):
        kept = []
        for block in range(supers):
            xa, xb = base_c[side * supers + block], base_s[side * supers + block]
            got = [jnp.zeros((8, LANES), F32)] * 4
            for k in range(4):
                c, s = rot_c[4 * side + k].astype(BF16), rot_s[4 * side + k].astype(BF16)
                moving = jnp.concatenate(
                    [spec_ref[j, near * block + q] for j in (3 - k, 4 + k) for q in range(near)], axis=0
                )
                waves = [jnp.concatenate(v, axis=1) for v in ([c * xa, s * xb], [c * xb, s * xa])]
                for w, wave in enumerate(waves):
                    both = jnp.dot(moving, wave, preferred_element_type=F32)
                    near_c, near_s = both[:, :LANES], both[:, LANES:]
                    for q in range(2 * near):
                        here = code == (8 * q + 3 - k if q < near else 8 * (q - near) + 4 + k)
                        for part in range(2):
                            at = slice(16 * q + 8 * part, 16 * q + 8 * part + 8)
                            if (w == 0) == (q < near):
                                value = near_c[at] + near_s[at]
                            else:
                                value = near_c[at] - near_s[at]
                            got[2 * w + part] = jnp.where(here, value, got[2 * w + part])
            got_re, got_im = got[0] - got[3], got[1] + got[2]
            kept.append(jnp.concatenate([got_re, got_im], axis=0))
        turned = jnp.transpose(jnp.concatenate(kept, axis=0))
        for d in range(some):
            pieces = [turned[u : u + 16] for u in range(d * gs, (d + 1) * gs, 16)]
            part_ref[side * some + d] = jnp.concatenate(pieces, axis=1).astype(BF16)
        flipped = [1 - v if side >> b & 1 else v for b, v in enumerate(bits)]
        base = sum(v * (fourth << b) for b, v in enumerate(flipped))
        for i in range(fourth):
            to = side * fourth + i
            slot = base
            for b, v in enumerate(low_bits):
                slot = slot + ((1 - v if i >> b & 1 else v) << b)

            @pl.when(to != me)
            def _():
                part_copy(slot, to).start()

    col = lax.broadcasted_iota(jnp.int32, (8, LANES), 1)
    t_c, t_s = cos_sin_turns(((col % 8) * row8).astype(F32) * 0.125)
    mix = jnp.where(col % 16 < 8, t_c, -t_s)[:, :32].astype(BF16)
    for copy in tables[1:]:
        copy.wait()
    totals = [part_ref[me * share + sub].astype(F32) for sub in range(share)]
    wait_all(got_part, part_recv)
    for step in range(n - 1, 0, -1):
        totals = [t + got_part[step, sub].astype(F32) for sub, t in enumerate(totals)]

    for sub in range(share):
        lower, upper = untangle(totals[sub][:8]), untangle(totals[sub][8:])
        zero_bin = jnp.logical_and(row8 == 0, jnp.logical_or(col == 0, col == 8))
        lower = jnp.where(zero_bin, 0.5 * lower, lower)
        bins = jnp.concatenate([lower, upper], axis=1).astype(BF16)
        a = jnp.dot(bins, inv_ref[...], preferred_element_type=F32)
        a_re, a_im = a[:, :window], a[:, window:]
        w_re, w_im = twist_ref[0:8, :], twist_ref[8:16, :]
        b = jnp.concatenate([a_re * w_re - a_im * w_im, a_re * w_im + a_im * w_re], axis=0)
        high = b.astype(BF16)
        low = (b - high.astype(F32)).astype(BF16)
        out = jnp.dot(mix, jnp.concatenate([high, low], axis=0), preferred_element_type=F32)
        out = out * (2.0 / (samples * math.sqrt(channels)))
        per = window // LANES
        for p in range(per):
            out_ref[sub, pl.ds(p, 8, stride=per), :] = out[:, p * LANES : (p + 1) * LANES]
    wait_all(got_part, send_sem)


def body(n, filterbank, channel_mask, band_edges, dm_delays):
    beams, local, samples = filterbank.shape
    channels = local * n
    bands = band_edges.shape[0] + 1
    trials = dm_delays.shape[0]
    share = trials // n
    window = samples // NBLK
    gs = PARTS * LANES // trials
    supers = samples // 32 // gs
    tab = forward_table(samples)
    inv, twist = inverse_tables(samples, gs)
    x = filterbank.reshape(local, samples)

    dma = pltpu.SemaphoreType.DMA
    series = pl.pallas_call(
        functools.partial(fused_kernel, n, bands, channels, trials),
        out_shape=jax.ShapeDtypeStruct((share, samples // LANES, LANES), F32),
        in_specs=[HBM] * 7,
        out_specs=VMEM,
        scratch_shapes=[
            pltpu.SMEM(band_edges.shape, jnp.int32),
            pltpu.SMEM(dm_delays.shape, jnp.int32),
            pltpu.VMEM((1, local), jnp.int32),
            pltpu.VMEM((local, samples), x.dtype),
            pltpu.VMEM(tab.shape, BF16),
            pltpu.VMEM(inv.shape, BF16),
            pltpu.VMEM(twist.shape, F32),
            pltpu.VMEM((local, NBLK * LANES), BF16),
            pltpu.VMEM((4 * PARTS, local, LANES), F32),
            pltpu.VMEM((4 * PARTS, local, LANES), F32),
            pltpu.VMEM((PARTS * supers, local, LANES), BF16),
            pltpu.VMEM((PARTS * supers, local, LANES), BF16),
            pltpu.VMEM((8, local, window), BF16),
            pltpu.VMEM((4, local, window), F32),
            pltpu.VMEM((8, samples // 256, 16, local), BF16),
            pltpu.VMEM((local, LANES), F32),
            pltpu.VMEM((1, LANES), F32),
            pltpu.VMEM((n, 1, LANES), F32),
            pltpu.VMEM((trials, 16, LANES), BF16),
            pltpu.VMEM((n, share, 16, LANES), BF16),
            pltpu.SemaphoreType.DMA((3,)), dma, dma, dma, dma,
        ],
        compiler_params=pltpu.CompilerParams(
            collective_id=0, has_side_effects=True, vmem_limit_bytes=24 << 20
        ),
    )(*[
        pltpu.with_memory_space_constraint(v, pltpu.HBM)
        for v in (
            band_edges, dm_delays, channel_mask.reshape(1, local), x,
            jnp.asarray(tab), jnp.asarray(inv), jnp.asarray(twist),
        )
    ])
    return series.reshape(beams, share, samples)


def solution(mesh):
    return jax.shard_map(
        functools.partial(body, mesh.shape["wide"]),
        mesh=mesh,
        in_specs=(P("beam", "wide", None), P(("beam", "wide")), P(), P()),
        out_specs=P("beam", "wide", None),
        check_vma=False,
    )
```
